32 devices in a mesh: samp: 32 (over z, y, x, core).
Axes of the slice: x: 2, y: 2, z: 4, core: 2. Of those that a mesh axis runs over, the one named last changes fastest.
Arguments:
- inputs: float32 [30, 65536], P(None, 'samp'), may hold values from -1 to 1
- response: float32 [32, 65536], P(None, 'samp')
- multi_index: int32 [5456, 30], replicated, may hold values from 0 to 3, as said below
- chosen: int32 [3], replicated, may hold values from 0 to 5455, as said below
Outputs:
- residual: float32 [32, 65536], P(None, 'samp')
- correlations: float32 [3, 32, 5456], replicated
- coefficients: float32 [3, 32], replicated
The draws below stay inside these ranges and needn't reach their ends.
Inputs may be any that keep to these rules, and one draw needn't show every extreme that they name: `multi_index`: rows are distinct; each row's degrees sum to 3 or less. `chosen`: distinct indices.
All inputs are finite; a program needn't handle non-finite values. Where the reference program divides by a largest or mean magnitude, that divisor is 1e-20 or more.
Results may differ from the reference program's by a relative error of at most 0.0062.
Values sent between devices are 32-bit elements; how exact they have to be, the bound alone decides.
A program may use at most 128 MiB of HBM per device.

```python
import math
import jax
import jax.numpy as jnp
import numpy as np
from jax import lax

NVARS = 30
CANDS = 5456
RESP = 32
ITERS = 3
SAMPLES = 65536


def enumerate_table(count):
    rows = [[0] * count]
    for first in range(count):
        for degree in range(1, 4):
            row = [0] * count
            row[first] = degree
            rows.append(row)
    for first in range(count):
        for second in range(first + 1, count):
            for pair in ((1, 1), (2, 1), (1, 2)):
                row = [0] * count
                row[first] = pair[0]
                row[second] = pair[1]
                rows.append(row)
    for first in range(count):
        for second in range(first + 1, count):
            for third in range(second + 1, count):
                row = [0] * count
                row[first] = 1
                row[second] = 1
                row[third] = 1
                rows.append(row)
    return np.array(rows, dtype=np.int32)


def factor_table_drawn(inputs):
    x = inputs
    one = jnp.ones_like(x)
    second = (3.0 * x * x - 1.0) * 0.5
    third = (5.0 * x * x * x - 3.0 * x) * 0.5
    stacked = jnp.stack([one, x * math.sqrt(3.0), second * math.sqrt(5.0), third * math.sqrt(7.0)], axis=1)
    return stacked.reshape(x.shape[0] * 4, x.shape[1])


def slot_index_drawn(multi_index):
    count = multi_index.shape[1]
    positive = multi_index > 0
    rank = jnp.cumsum(positive.astype(jnp.int32), axis=1) - 1
    flat_pos = jnp.arange(count, dtype=jnp.int32)[None, :] * 4 + multi_index
    result = []
    for slot in range(3):
        picked = jnp.logical_and(positive, rank == slot)
        result.append(jnp.sum(jnp.where(picked, flat_pos, 0), axis=1).astype(jnp.int32))
    return tuple(result)


def draw_multi_index(key, part):
    table = jnp.asarray(enumerate_table(NVARS))
    order = jax.random.permutation(jax.random.fold_in(key, 11), CANDS)
    columns = jax.random.permutation(jax.random.fold_in(key, 12), NVARS)
    return table[order][:, columns].astype(jnp.int32)


def draw_chosen(key, part):
    middle = 1 + jax.random.permutation(jax.random.fold_in(key, 13), CANDS - 2)[:ITERS - 2]
    ends = jnp.array([0, CANDS - 1], dtype=jnp.int32)
    picks = jnp.concatenate([ends, middle.astype(jnp.int32)])
    order = jax.random.permutation(jax.random.fold_in(key, 19), ITERS)
    return picks[order].astype(jnp.int32)


def shared_data(key):
    uniform_x = jax.random.uniform(jax.random.fold_in(key, 14), (NVARS, SAMPLES), jnp.float32, -1.0, 1.0)
    inputs = uniform_x
    multi = draw_multi_index(key, 0)
    picks = draw_chosen(key, 0)
    flat = factor_table_drawn(inputs)
    index = slot_index_drawn(multi)
    active = jnp.take(flat, index[0][picks], axis=0) * jnp.take(flat, index[1][picks], axis=0) * jnp.take(flat, index[2][picks], axis=0)
    size = jax.random.uniform(jax.random.fold_in(key, 15), (ITERS, RESP), jnp.float32, 0.5, 2.0)
    flips = jax.random.randint(jax.random.fold_in(key, 16), (ITERS, RESP), 0, 2) * 2 - 1
    amps = size * flips.astype(jnp.float32)
    ramp = 1.0 + 2.0 * jnp.arange(SAMPLES, dtype=jnp.float32) / SAMPLES
    noise = jax.random.normal(jax.random.fold_in(key, 17), (RESP, SAMPLES), jnp.float32) * ramp * 0.5
    response = jnp.dot(amps.T, active, precision=jax.lax.Precision.HIGHEST) + noise
    return (inputs, response)


def draw_inputs(key, part):
    return shared_data(key)[0]


def draw_response(key, part):
    return shared_data(key)[1]


def setup_inputs(seed: int = 0) -> dict:
    arg_keys = jax.random.split(jax.random.key(seed), 5)
    inputs = draw_inputs(jax.random.fold_in(arg_keys[4], 71), 0)
    response = draw_response(jax.random.fold_in(arg_keys[4], 71), 0)
    multi_index = draw_multi_index(jax.random.fold_in(arg_keys[4], 71), 0)
    chosen = draw_chosen(jax.random.fold_in(arg_keys[4], 71), 0)
    return {"inputs": inputs, "response": response, "multi_index": multi_index, "chosen": chosen}


def factor_table(inputs):
    x = inputs
    one = jnp.ones_like(x)
    second = (3.0 * x * x - 1.0) * 0.5
    third = (5.0 * x * x * x - 3.0 * x) * 0.5
    stacked = jnp.stack([one, x * math.sqrt(3.0), second * math.sqrt(5.0), third * math.sqrt(7.0)], axis=1)
    return stacked.reshape(x.shape[0] * 4, x.shape[1])

def slot_index(multi_index):
    count = multi_index.shape[1]
    positive = multi_index > 0
    rank = jnp.cumsum(positive.astype(jnp.int32), axis=1) - 1
    flat_pos = jnp.arange(count, dtype=jnp.int32)[None, :] * 4 + multi_index
    result = []
    for slot in range(3):
        picked = jnp.logical_and(positive, rank == slot)
        result.append(lax.optimization_barrier(jnp.sum(jnp.where(picked, flat_pos, 0), axis=1)).astype(jnp.int32))
    return tuple(result)

def design(flat, index):
    first = jnp.take(flat, index[0], axis=0)
    second = jnp.take(flat, index[1], axis=0)
    third = jnp.take(flat, index[2], axis=0)
    return (first * second * third).astype(jnp.bfloat16)

def reference(inputs, response, multi_index, chosen):
    samples = inputs.shape[1]
    cands = multi_index.shape[0]
    iters = chosen.shape[0]
    resp = response.shape[0]
    flat = factor_table(inputs)
    index = slot_index(multi_index)
    active = design(flat, tuple((i[chosen] for i in index)))
    gram = jnp.dot(active.astype(jnp.float32), active.T.astype(jnp.float32), preferred_element_type=jnp.float32)
    width = math.gcd(samples, 4096)
    nblocks = samples // width

    def correlate(rb):

        def step(i, acc):
            piece = lax.dynamic_slice_in_dim(flat, i * width, width, 1)
            part = lax.dynamic_slice_in_dim(rb, i * width, width, 1)
            psi = design(piece, index)
            return acc + lax.dot_general(part.astype(jnp.float32), psi.astype(jnp.float32), (((1,), (1,)), ((), ())), preferred_element_type=jnp.float32)
        return lax.fori_loop(0, nblocks, step, jnp.zeros((resp, cands), jnp.float32))
    residual = response
    coefs = jnp.zeros((iters, resp), jnp.float32)
    outs = []
    for k in range(iters):
        rb = residual.astype(jnp.bfloat16)
        corr = correlate(rb)
        sq = lax.optimization_barrier(jnp.sum(residual * residual, axis=1))
        norm = math.sqrt(samples) * jnp.sqrt(sq / samples + 1e-06)
        outs.append(corr / norm[:, None])
        largest = lax.optimization_barrier(jnp.max(jnp.abs(corr), axis=1))
        gamma = jnp.abs(corr[:, chosen[k]]) / (largest + 1e-06)
        factor = jnp.linalg.cholesky(gram[:k + 1, :k + 1])
        target = corr[:, chosen[:k + 1]].T
        weights = jax.scipy.linalg.cho_solve((factor, True), target)
        update = jnp.dot(weights.T, active[:k + 1].astype(jnp.float32), precision=lax.Precision.HIGHEST)
        residual = residual - gamma[:, None] * update
        coefs = coefs.at[:k + 1].add(weights * gamma[None, :])
    return (residual, jnp.stack(outs), coefs)
```

```python
import functools
import math

import jax
import jax.numpy as jnp
from jax import lax
from jax.experimental import pallas as pl
from jax.experimental.pallas import tpu as pltpu
from jax.sharding import PartitionSpec as P

TILE = 512
NT = (((1,), (1,)), ((), ()))


def up(n, m):
    return -(-n // m) * m


def slots(multi, stride):
    degree = multi.astype(jnp.float32)
    var = lax.broadcasted_iota(jnp.int32, multi.shape, 1).astype(jnp.float32)
    positive = degree > 0.0
    code = degree * float(stride) + var
    count = jnp.sum(jnp.where(positive, 1.0, 0.0), axis=1, keepdims=True)
    total = jnp.sum(jnp.where(positive, code, 0.0), axis=1, keepdims=True)
    high = jnp.max(jnp.where(positive, code, 0.0), axis=1, keepdims=True)
    low = jnp.min(jnp.where(positive, code, 1e6), axis=1, keepdims=True)
    low = jnp.where(count > 0.5, low, 0.0)
    second = jnp.where(count > 1.5, high, 0.0)
    third = jnp.where(count > 2.5, total - low - high, 0.0)
    return low, second, third


def picks(multi, stride):
    levels = 4 * stride
    column = lax.broadcasted_iota(jnp.int32, (multi.shape[0], 2 * levels), 1)
    column = jnp.where(column >= levels, column - levels, column).astype(jnp.float32)
    return jnp.concatenate(
        [jnp.where(column == s, 1.0, 0.0) for s in slots(multi, stride)], axis=0
    ).astype(jnp.bfloat16)


def product(onehot, table):
    rows = onehot.shape[0] // 3
    f = jnp.dot(onehot, table, preferred_element_type=jnp.float32)
    return (f[:rows] * f[rows : 2 * rows] * f[2 * rows :]).astype(jnp.bfloat16)


def split(x):
    high = x.astype(jnp.bfloat16)
    return high, (x - high.astype(jnp.float32)).astype(jnp.bfloat16)


def correlate(cands, stride, chunk, x_ref, res_ref, few_ref, multi_ref, out_ref, active_ref, table, rows):
    step = pl.program_id(0)
    resp, width = res_ref.shape
    levels = 4 * stride
    chunks = [slice(i, i + chunk) for i in range(0, width, chunk)]

    @pl.when(step == 0)
    def _():
        x = x_ref[...]
        second = (3.0 * x * x - 1.0) * 0.5
        third = (5.0 * x * x * x - 3.0 * x) * 0.5
        values = [jnp.ones_like(x), x * math.sqrt(3.0), second * math.sqrt(5.0), third * math.sqrt(7.0)]
        for d, value in enumerate(values):
            high, low = split(value)
            table[d * stride : (d + 1) * stride, :] = high
            table[levels + d * stride : levels + (d + 1) * stride, :] = low
        high, low = split(res_ref[...])
        rows[0:resp, :] = high
        rows[resp : 2 * resp, :] = low
        onehot = picks(few_ref[...], stride)
        for c in chunks:
            active = product(onehot, table[:, c])
            rows[2 * resp :, c] = active
            active_ref[:, c] = active

    onehot = picks(multi_ref[...], stride)
    acc = jnp.zeros((multi_ref.shape[0], rows.shape[0]), jnp.float32)
    for c in chunks:
        psi = product(onehot, table[:, c])
        acc += lax.dot_general(psi, rows[:, c], NT, preferred_element_type=jnp.float32)
    turned = acc.T
    out_ref[0:resp, :] = turned[0:resp] + turned[resp : 2 * resp]
    out_ref[resp:, :] = turned[2 * resp : 2 * resp + out_ref.shape[0] - resp]

    @pl.when(step == pl.num_programs(0) - 1)
    def _():
        res = res_ref[...]
        sq = jnp.sum(res * res, axis=1, keepdims=True)
        tail = out_ref[0:resp, TILE - 128 :]
        lane = lax.broadcasted_iota(jnp.int32, tail.shape, 1)
        out_ref[0:resp, TILE - 128 :] = jnp.where(lane == 127, sq, tail)


def finish(cands, samples, iters, chosen_ref, total_ref, res_ref, active_ref, out_ref, corr_ref, coef_ref):
    resp = res_ref.shape[0]
    total = total_ref[...]
    column = lax.broadcasted_iota(jnp.int32, total.shape, 1)
    picked = [
        jnp.sum(jnp.where(column == chosen_ref[i], total, 0.0), axis=1, keepdims=True)
        for i in range(iters)
    ]
    target = [p[0:resp] for p in picked]
    gram = [[picked[j][resp + i : resp + i + 1] for j in range(iters)] for i in range(iters)]
    sq = total[0:resp, total.shape[1] - 1 :]
    tri = [[None] * iters for _ in range(iters)]
    for i in range(iters):
        for j in range(i + 1):
            s = gram[i][j]
            for m in range(j):
                s = s - tri[i][m] * tri[j][m]
            tri[i][j] = jnp.sqrt(s) if i == j else s / tri[j][j]
    corr = total[0:resp, 0:cands]
    rows = [total[resp + i : resp + i + 1, 0:cands] for i in range(iters)]
    coef = [jnp.zeros((resp, 1), jnp.float32) for _ in range(iters)]
    for k in range(iters):
        norm = math.sqrt(samples) * jnp.sqrt(sq / samples + 1e-06)
        corr_ref[k] = corr * (1.0 / norm)
        largest = jnp.max(jnp.abs(corr), axis=1, keepdims=True)
        gamma = jnp.abs(target[k]) / (largest + 1e-06)
        w = []
        for i in range(k + 1):
            s = target[i]
            for m in range(i):
                s = s - tri[i][m] * w[m]
            w.append(s / tri[i][i])
        for i in reversed(range(k + 1)):
            s = w[i]
            for m in range(i + 1, k + 1):
                s = s - tri[m][i] * w[m]
            w[i] = s / tri[i][i]
        step = [gamma * wi for wi in w]
        for i in range(k + 1):
            coef[i] = coef[i] + step[i]
        if k < iters - 1:
            gain = sum(wi * t for wi, t in zip(w, target))
            sq = jnp.maximum(sq - gamma * (2.0 - gamma) * gain, 0.0)
            target = [
                target[j] - sum(step[i] * gram[i][j] for i in range(k + 1)) for j in range(iters)
            ]
            for i in range(k + 1):
                corr = corr - step[i] * rows[i]
    res = res_ref[...]
    active = active_ref[...].astype(jnp.float32)
    for i in range(iters):
        res = res - coef[i] * active[i : i + 1]
    out_ref[...] = res
    shape = (resp, resp)
    eye = lax.broadcasted_iota(jnp.int32, shape, 0) == lax.broadcasted_iota(jnp.int32, shape, 1)
    lines = [jnp.sum(jnp.where(eye, c, 0.0), axis=0, keepdims=True) for c in coef]
    line = lax.broadcasted_iota(jnp.int32, coef_ref.shape, 0)
    coef_ref[...] = sum(jnp.where(line == i, lines[i], 0.0) for i in range(iters))


def on_device(inputs, response, multi_index, chosen):
    nvars, width = inputs.shape
    samples = width * lax.axis_size("samp")
    cands = multi_index.shape[0]
    iters = chosen.shape[0]
    resp = response.shape[0]
    stride = up(nvars, 16)
    few = up(iters, 16)
    extra = up(iters, 8)
    padded = up(cands + 1, TILE)
    chunk = math.gcd(width, 256)
    x = jnp.pad(inputs, ((0, stride - nvars), (0, 0)))
    picked = jnp.pad(multi_index[chosen], ((0, few - iters), (0, 0)))
    whole = lambda shape: pl.BlockSpec(shape, lambda i: (0, 0))
    local, active = pl.pallas_call(
        functools.partial(correlate, cands, stride, chunk),
        grid=(padded // TILE,),
        in_specs=[
            whole((stride, width)),
            whole((resp, width)),
            whole((few, nvars)),
            pl.BlockSpec((TILE, nvars), lambda i: (i, 0)),
        ],
        out_specs=[pl.BlockSpec((resp + extra, TILE), lambda i: (0, i)), whole((few, width))],
        out_shape=[
            jax.ShapeDtypeStruct((resp + extra, padded), jnp.float32),
            jax.ShapeDtypeStruct((few, width), jnp.bfloat16),
        ],
        scratch_shapes=[
            pltpu.VMEM((8 * stride, width), jnp.bfloat16),
            pltpu.VMEM((2 * resp + few, width), jnp.bfloat16),
        ],
        compiler_params=pltpu.CompilerParams(
            dimension_semantics=("arbitrary",), vmem_limit_bytes=48 * 2**20
        ),
        name="correlate",
    )(x, response, picked, jnp.pad(multi_index, ((0, padded - cands), (0, 0))))
    total = lax.psum(local, "samp")
    vmem = pl.BlockSpec(memory_space=pltpu.VMEM)
    residual, corr, coef = pl.pallas_call(
        functools.partial(finish, cands, samples, iters),
        in_specs=[pl.BlockSpec(memory_space=pltpu.SMEM), vmem, vmem, vmem],
        out_specs=[vmem, vmem, vmem],
        out_shape=[
            jax.ShapeDtypeStruct((resp, width), jnp.float32),
            jax.ShapeDtypeStruct((iters, resp, cands), jnp.float32),
            jax.ShapeDtypeStruct((extra, resp), jnp.float32),
        ],
        compiler_params=pltpu.CompilerParams(vmem_limit_bytes=48 * 2**20),
        name="finish",
    )(chosen, total, response, active)
    return residual, corr, coef[:iters]


def solution(mesh):
    placed = (P(None, "samp"), P(None, "samp"), P(), P())
    return jax.shard_map(
        on_device,
        mesh=mesh,
        in_specs=placed,
        out_specs=(P(None, "samp"), P(), P()),
        check_vma=False,
    )
```
